1024 devices in a mesh: gx: 32 (over x, y, core), gy: 32 (over z).
Axes of the slice: x: 4, y: 4, z: 32, core: 2. Of those that a mesh axis runs over, the one named last changes fastest.
Arguments:
- fields: float32 [4, 512, 512, 128], P(None, 'gx', 'gy'), may hold values from -6 to 6
- factor_x: float32 [512, 32], P('gx'), may hold values from -0.5 to 0.5
- factor_y: float32 [512, 32], P('gy'), may hold values from -0.5 to 0.5
Outputs:
- advanced: float32 [4, 512, 512, 128], P(None, 'gx', 'gy')
- core_tensor: float32 [4, 32, 32, 128], P(None, 'gx', 'gy')
- rebuilt: float32 [4, 512, 512, 128], P(None, 'gx', 'gy')
The draws below stay inside these ranges and needn't reach their ends.
All inputs are finite; a program needn't handle non-finite values.
Results may differ from the reference program's by a relative error of at most 0.000082.
Values sent between devices are 32-bit elements; how exact they have to be, the bound alone decides.
A program may use at most 32 MiB of HBM per device.

```python
import jax
import jax.numpy as jnp
from jax import lax

NZ = 128
RANK = 32
FIELDS = 4
NX = 512
NY = 512


def strengthened(result, own_key, source, target, shards_of, factor):
    def block_of(position):
        return (jnp.arange(result.shape[position]) // (result.shape[position] // shards_of)).reshape((-1,) + (1,) * (result.ndim - 1 - position))

    one_side = jax.random.permutation(own_key, shards_of)[block_of(target)]
    second = (block_of(target) + shards_of // 2) % shards_of
    return jnp.where((block_of(source) == one_side) | (block_of(source) == second), factor * result, result)


def levels(rng, extent, shards, least, top_value):
    gain = 1.0
    for dim, shards_of in shards:
        steps = jax.random.uniform(jax.random.fold_in(jax.random.fold_in(rng, 6), dim), (shards_of,), jnp.float32, least / len(shards), top_value / len(shards))
        gain = gain * jnp.repeat(jnp.exp(steps), extent[dim] // shards_of).reshape((-1,) + (1,) * (len(extent) - 1 - dim))
    return gain


def noise(key, shape, spread, bound, pieces=(), dtype=jnp.bfloat16):
    entries = spread * jax.random.normal(key, shape, jnp.float32)
    if pieces:
        entries = entries * levels(key, shape, pieces, -0.22, 0.18)
    return jnp.clip(entries, -bound, bound).astype(dtype)


def heavy_noise(key, extent, width, most, cuts, heavy, dtype=jnp.bfloat16):
    drawn = width * jax.random.normal(key, extent, jnp.float32)
    if cuts:
        drawn = drawn * levels(key, extent, cuts, -0.22, 0.18)
    return jnp.clip(strengthened(drawn, jax.random.fold_in(key, 3), *heavy), -most, most).astype(dtype)


def setup_inputs(seed: int = 0) -> dict:
    splits = jax.random.split(jax.random.key(seed), 4)
    return {
        "fields": noise(splits[0], (FIELDS, NX, NY, NZ), 1.0, 6.0, ((1, 32), (2, 32)), jnp.float32),
        "factor_x": heavy_noise(splits[1], (NX, RANK), NX ** -0.5, 0.5, ((0, 32),), (0, 1, 32, 2.75), jnp.float32),
        "factor_y": heavy_noise(splits[2], (NY, RANK), NY ** -0.5, 0.5, ((0, 32),), (0, 1, 32, 2.75), jnp.float32),
    }


TIME_STEP = 0.2
REACT_RATE = 0.5
HEAT_RELEASE = 1.0


def derivative(flux_field, axis):
    def pair(shift):
        return jnp.roll(flux_field, -shift, axis) - jnp.roll(flux_field, shift, axis)
    return (45.0 * pair(1) - 9.0 * pair(2) + pair(3)) / 60.0


def tendency(state):
    pressure = 0.5 * state[3]
    flux_x = state[0][None] * state
    flux_x = flux_x.at[0].add(pressure)
    flux_y = state[1][None] * state
    flux_y = flux_y.at[1].add(pressure)
    react = REACT_RATE * state[2] * (1.0 + jnp.tanh(state[3]))
    zeros = jnp.zeros_like(react)
    source = jnp.stack([zeros, zeros, -react, HEAT_RELEASE * react])
    return source - derivative(flux_x, 1) - derivative(flux_y, 2)


def reference(fields, factor_x, factor_y):
    high = lax.Precision.HIGHEST
    z_width = min(NZ, 16)
    n_blocks = NZ // z_width
    rescale = (float(NX) * float(NY)) ** 0.5 / RANK

    def one_block(state):
        section_one = state + TIME_STEP * tendency(state)
        section_two = 0.75 * state + 0.25 * (section_one + TIME_STEP * tendency(section_one))
        advanced = (1.0 / 3.0) * state + (2.0 / 3.0) * (section_two + TIME_STEP * tendency(section_two))
        partial_value = jnp.einsum("fxyz,xa->fayz", advanced, factor_x, precision=high)
        core_tensor = jnp.einsum("fayz,yb->fabz", partial_value, factor_y, precision=high)
        columns = jnp.einsum("fabz,yb->fayz", core_tensor, factor_y, precision=high)
        rebuilt = rescale * jnp.einsum("fayz,xa->fxyz", columns, factor_x, precision=high)
        return advanced, core_tensor, rebuilt

    blocks = jnp.moveaxis(fields.reshape(FIELDS, NX, NY, n_blocks, z_width), 3, 0)
    adv_blocks, core_blocks, rebuilt_blocks = lax.map(one_block, blocks)

    def joined(stacked):
        shape = stacked.shape
        return jnp.moveaxis(stacked, 0, 3).reshape(shape[1], shape[2], shape[3], NZ)

    return joined(adv_blocks), joined(core_blocks), joined(rebuilt_blocks)
```

```python
import functools
import math

import jax
import jax.numpy as jnp
from jax import lax
from jax.experimental import pallas as pl
from jax.experimental.pallas import tpu as pltpu
from jax.sharding import PartitionSpec as P

TIME_STEP = 0.2
REACT_RATE = 0.5
HEAT_RELEASE = 1.0
HIGH = lax.Precision.HIGHEST
SECTIONS = ((0.0, 1.0), (0.75, 0.25), (1.0 / 3.0, 2.0 / 3.0))
LOW, TOP = 0, 1
N = 16
F = 4
W = 3
RANK = 32
CHIPS = 16
CHUNKS = 2
FC = F // CHUNKS


def far_first(count):
    order = []
    for k in range(count // 2, 0, -1):
        order += [k] if 2 * k == count else [k, count - k]
    return order


Z_ORDER = far_first(32)


def in_plane_order():
    def hops(k):
        y, x = k % 4, k // 4
        return min(y, 4 - y) + min(x, 4 - x)

    return sorted(range(1, CHIPS), key=lambda k: -hops(k))


PLANE_ORDER = in_plane_order()


def iota(shape, dim):
    return lax.broadcasted_iota(jnp.int32, shape, dim)


def dot(a, b, contract=((1,), (0,))):
    return lax.dot_general(
        a, b, (contract, ((), ())), precision=HIGH, preferred_element_type=jnp.float32
    )


def one_hot(hit):
    return jnp.where(hit, 1.0, 0.0).astype(jnp.float32)


def spread(rows, cells):
    n, k = rows.shape
    wide = dot(rows, one_hot(iota((k, 8 * k), 1) // 8 == iota((k, 8 * k), 0)))
    same = iota((n, 8 * k), 0) % 8 == iota((n, 8 * k), 1) % 8
    return jnp.where(same, wide, 0.0)


def kernel(
    rescale,
    fields, fx, fy,
    adv, core_out, reb,
    state, flux_x, flux_y, halo_x, halo_y, edge_y,
    mate_adv, fx_own, fx_mate, part, part_in, local, core_in, core_own, core_all, cols, gathered,
    lhs_in, lhs_out, fy_t,
    load_sem, halo_send, halo_recv, fx_sems, mate_send, mate_recv,
    plane_send, plane_recv, z_send, z_recv, zb_send, zb_recv, back_send, back_recv, pass_send, pass_recv,
    near_sem,
):
    gx, gy = lax.axis_index("gx"), lax.axis_index("gy")
    core = lax.rem(gx, 2)
    mate = {"gx": gx + 1 - 2 * core}

    def along(axis, offset):
        count, me = 32, (gx if axis == "gx" else gy)
        return {axis: lax.rem(me + (offset + count), count)}

    def signal(sem, target):
        pl.semaphore_signal(sem, inc=1, device_id=target, device_id_type=pl.DeviceIdType.MESH)

    def copy(src, dst, send, recv, target):
        return pltpu.make_async_remote_copy(
            src_ref=src, dst_ref=dst, send_sem=send, recv_sem=recv,
            device_id=target, device_id_type=pl.DeviceIdType.MESH,
        )

    def take_all(sem, ref):
        pltpu.make_async_copy(ref, ref, sem).wait()

    load = pltpu.make_async_copy(fields, state.at[0], load_sem)
    load.start()
    barrier = pltpu.get_barrier_semaphore()
    for axis in ("gx", "gy"):
        for side in (-1, 1):
            signal(barrier, along(axis, side))

    fx_own[...] = jnp.zeros_like(fx_own)
    fx_own[:, 0:RANK] = fx[...]
    zero_rows = jnp.zeros((8, 128), jnp.float32)

    @pl.loop(0, N)
    def _(x):
        for f in range(F):
            flux_y[f, x, 0:8, :] = zero_rows
            flux_y[f, x, 24:32, :] = zero_rows

    pl.semaphore_wait(barrier, 4)

    def sign_in(level):
        for i, axis in enumerate(("gx", "gy")):
            for side in (-1, 1):
                signal(near_sem.at[i, level], along(axis, side * (1 << level)))

    def signed_in(level):
        for i in range(2):
            pl.semaphore_wait(near_sem.at[i, level], 2)

    sign_in(0)
    fx_copy = copy(fx_own, fx_mate, fx_sems.at[0], fx_sems.at[1], mate)
    fx_copy.start()
    load.wait()

    def flat(s):
        return (adv if s == 3 else state.at[s]).reshape(F * N * N, 128)

    for f in range(F):
        for j in range(W):
            edge_y[0, LOW, f, j] = flat(0)[pl.ds(f * N * N + j, N, stride=N), :]
            edge_y[0, TOP, f, j] = flat(0)[pl.ds(f * N * N + N - W + j, N, stride=N), :]

    def halo_copies(s):
        now = state.at[s]
        return (
            copy(edge_y.at[s, LOW], halo_y.at[s, TOP], halo_send.at[s, 0], halo_recv.at[s, 0], along("gy", -1)),
            copy(edge_y.at[s, TOP], halo_y.at[s, LOW], halo_send.at[s, 1], halo_recv.at[s, 1], along("gy", 1)),
            copy(now.at[:, pl.ds(0, W)], halo_x.at[s, TOP], halo_send.at[s, 2], halo_recv.at[s, 2], along("gx", -1)),
            copy(now.at[:, pl.ds(N - W, W)], halo_x.at[s, LOW], halo_send.at[s, 3], halo_recv.at[s, 3], along("gx", 1)),
        )

    def fluxes(values, which):
        total = [values[which] * v for v in values]
        total[which] = total[which] + 0.5 * values[3]
        return total

    def section(s):
        keep, take = SECTIONS[s]
        now, base = state.at[s], state.at[0]
        after = adv if s == 2 else state.at[s + 1]
        copies = halo_copies(s)
        for c in copies:
            c.start()

        @pl.loop(0, N)
        def _(x):
            for t in range(2):
                rows = pl.ds(8 * t, 8)
                values = [now[f, x, rows, :] for f in range(F)]
                for f, g in enumerate(fluxes(values, 0)):
                    flux_x[f, x + W, rows, :] = g
                for f, g in enumerate(fluxes(values, 1)):
                    flux_y[f, x, pl.ds(8 + 8 * t, 8), :] = g

        scale = take * TIME_STEP / 60.0

        def advance(x):
            for t in range(2):
                rows = pl.ds(8 * t, 8)
                heat = now[3, x, rows, :]
                react = (take * TIME_STEP * REACT_RATE) * now[2, x, rows, :] * (1.0 + jnp.tanh(heat))
                for f in range(F):
                    def pair(shift):
                        in_x = flux_x[f, x + (W + shift), rows, :] - flux_x[f, x + (W - shift), rows, :]
                        start = 8 + 8 * t
                        in_y = flux_y[f, x, pl.ds(start + shift, 8), :] - flux_y[f, x, pl.ds(start - shift, 8), :]
                        return in_x + in_y

                    slope = (45.0 * scale) * pair(1) - (9.0 * scale) * pair(2) + scale * pair(3)
                    new = take * now[f, x, rows, :] - slope
                    if keep:
                        new = new + keep * base[f, x, rows, :]
                    if f == 2:
                        new = new - react
                    if f == 3:
                        new = new + HEAT_RELEASE * react
                    after[f, x, rows, :] = new

        @pl.loop(W, N - W)
        def _(x):
            advance(x)

        if s < 2:
            signed_in(s)
            sign_in(s + 1)
        copies[2].wait_recv()
        copies[3].wait_recv()
        for side, first in ((LOW, 0), (TOP, N + W)):
            @pl.loop(0, W)
            def _(j):
                for t in range(2):
                    rows = pl.ds(8 * t, 8)
                    values = [halo_x[s, side, f, j, rows, :] for f in range(F)]
                    for f, g in enumerate(fluxes(values, 0)):
                        flux_x[f, first + j, rows, :] = g

        @pl.loop(0, W)
        def _(j):
            advance(j)
            advance(N - W + j)

        if s == 1:
            signed_in(2)
            sign_in(3)
        copies[0].wait_recv()
        copies[1].wait_recv()
        out = flat(s + 1)
        for side in (LOW, TOP):
            sign = 1.0 if side == LOW else -1.0
            near = (2, 1, 0) if side == LOW else (0, 1, 2)
            flux = []
            for j in near:
                flux.append(fluxes([halo_y[s, side, f, j] for f in range(F)], 1))
            for f in range(F):
                g1, g2, g3 = (flux[k][f] for k in range(W))
                changes = (
                    (sign * 45.0 * scale) * g1 - (sign * 9.0 * scale) * g2 + (sign * scale) * g3,
                    (sign * scale) * g2 - (sign * 9.0 * scale) * g1,
                    (sign * scale) * g1,
                )
                for k, change in enumerate(changes):
                    y = k if side == LOW else N - 1 - k
                    at = pl.ds(f * N * N + y, N, stride=N)
                    new = out[at, :] + change
                    out[at, :] = new
                    if s < 2:
                        edge_y[s + 1, side, f, k if side == LOW else W - 1 - k] = new
        return copies

    sent = []
    sent += section(0)
    fx_copy.wait_recv()
    picked = one_hot(iota((128, RANK), 1) == 2 * (iota((128, RANK), 0) // 8) + core)
    for half, factor in ((0, fx_own), (1, fx_mate)):
        rows = dot(picked, factor[:, 0:RANK], ((1,), (1,)))
        lhs_in[:, 128 * half : 128 * half + 128] = spread(rows, N)
    rows = dot(one_hot(iota((128, N), 0) // 8 == iota((128, N), 1)), fx_own[:, 0:RANK])
    lhs_out[...] = rescale * spread(rows, RANK)
    fy_t[...] = dot(one_hot(iota((RANK, RANK), 0) == iota((RANK, RANK), 1)), fy[...], ((1,), (1,)))
    sent += section(1)
    sent += section(2)

    mates = []
    for c in range(CHUNKS):
        piece = pl.ds(c * FC, FC)
        mates.append(copy(adv.at[piece], mate_adv.at[piece], mate_send.at[c], mate_recv.at[c], mate))
        mates[-1].start()
    signed_in(3)
    sent += mates

    def tiles(ref, f):
        return jnp.concatenate(
            [ref[f, :, 8 * t : 8 * t + 8, :].reshape(8 * N, 128) for t in range(2)], axis=1
        )

    chip = gx // 2
    plane = []
    for c in range(CHUNKS):
        mates[c].wait_recv()
        for i in range(FC):
            f = c * FC + i
            both = jnp.concatenate([tiles(adv, f), tiles(mate_adv, f)], axis=0)
            total = dot(lhs_in[...], both)
            for t in range(2):
                part[c, :, i, 8 * t : 8 * t + 8, :] = total[:, 128 * t : 128 * t + 128].reshape(CHIPS, 8, 128)
        for k in PLANE_ORDER:
            to = lax.rem(chip + k, CHIPS)
            plane.append(
                copy(part.at[c, to], part_in.at[c, k - 1], plane_send.at[c], plane_recv.at[c], {"gx": 2 * to + core})
            )
            plane[-1].start()

    out_z = []
    for c in range(CHUNKS):
        take_all(plane_recv.at[c], part_in.at[c])
        for i in range(FC):
            total = part[c, chip, i]
            for k in range(CHIPS - 1):
                total = total + part_in[c, k, i]
            local[c, :, i, :] = dot(fy_t[...], total)
        for k in Z_ORDER:
            to = lax.rem(gy + k, 32)
            out_z.append(copy(local.at[c, to], core_in.at[c, k - 1], z_send.at[c], z_recv.at[c], {"gy": to}))
            out_z[-1].start()

    back_z = []
    for c in range(CHUNKS):
        take_all(z_recv.at[c], core_in.at[c])
        total = local[c, gy]
        for k in range(31):
            total = total + core_in[c, k]
        core_own[c] = total
        core_all[c, gy] = total
        core_out[c * FC : c * FC + FC, :] = total
        for k in Z_ORDER:
            to = lax.rem(gy + k, 32)
            back_z.append(copy(core_own.at[c], core_all.at[c, gy], zb_send.at[c], zb_recv.at[c], {"gy": to}))
            back_z[-1].start()

    back = []
    passed = []
    for c in range(CHUNKS):
        take_all(zb_recv.at[c], core_all.at[c, pl.ds(0, 31)])
        for i in range(FC):
            expanded = dot(fy[...], core_all[c, :, i, :])
            cols[c, i] = expanded
            gathered[c, gx, i] = expanded
        for k in PLANE_ORDER:
            to = lax.rem(chip + k, CHIPS)
            back.append(
                copy(cols.at[c], gathered.at[c, gx], back_send.at[c], back_recv.at[c, k - 1], {"gx": 2 * to + core})
            )
            back[-1].start()
        passed.append(copy(cols.at[c], gathered.at[c, gx], pass_send.at[c], pass_recv.at[c], mate))
        passed[-1].start()
    for c in range(CHUNKS):
        for n, k in reversed(list(enumerate(PLANE_ORDER))):
            back[c * (CHIPS - 1) + n].wait_recv()
            came = 2 * lax.rem(chip + (CHIPS - k), CHIPS) + core
            passed.append(
                copy(gathered.at[c, came], gathered.at[c, came], pass_send.at[c], pass_recv.at[c], mate)
            )
            passed[-1].start()
    for c in range(CHUNKS):
        take_all(pass_recv.at[c], gathered.at[c, pl.ds(0, CHIPS)])
        for i in range(FC):
            both = jnp.concatenate(
                [gathered[c, :, i, 8 * t : 8 * t + 8, :].reshape(8 * RANK, 128) for t in range(2)], axis=1
            )
            whole = dot(lhs_out[...], both)
            for t in range(2):
                reb[c * FC + i, :, 8 * t : 8 * t + 8, :] = whole[:, 128 * t : 128 * t + 128].reshape(N, 8, 128)

    for c in sent + [fx_copy]:
        c.wait_send()
    for c in range(CHUNKS):
        take_all(plane_send.at[c], part_in.at[c])
        take_all(z_send.at[c], core_in.at[c])
        take_all(zb_send.at[c], core_all.at[c, pl.ds(0, 31)])
        take_all(back_send.at[c], gathered.at[c, pl.ds(0, CHIPS - 1)])
        take_all(pass_send.at[c], gathered.at[c, pl.ds(0, CHIPS)])


def per_device(fields, factor_x, factor_y):
    total_x, total_y = factor_x.shape[0] * 32, factor_y.shape[0] * 32
    rescale = math.sqrt(float(total_x) * float(total_y)) / factor_x.shape[1]
    f32 = jnp.float32
    vmem = pltpu.VMEM
    dma = pltpu.SemaphoreType.DMA
    whole = (F, N, N, 128)
    scratch = [
        vmem((3, *whole), f32),
        vmem((F, N + 2 * W, N, 128), f32),
        vmem((F, N, 2 * N, 128), f32),
        vmem((3, 2, F, W, N, 128), f32),
        vmem((3, 2, F, W, N, 128), f32),
        vmem((3, 2, F, W, N, 128), f32),
        vmem(whole, f32),
        vmem((N, 128), f32),
        vmem((N, 128), f32),
        vmem((CHUNKS, CHIPS, FC, N, 128), f32),
        vmem((CHUNKS, CHIPS - 1, FC, N, 128), f32),
        vmem((CHUNKS, RANK, FC, 128), f32),
        vmem((CHUNKS, 31, FC, 128), f32),
        vmem((CHUNKS, FC, 128), f32),
        vmem((CHUNKS, RANK, FC, 128), f32),
        vmem((CHUNKS, FC, N, 128), f32),
        vmem((CHUNKS, RANK, FC, N, 128), f32),
        vmem((128, 256), f32),
        vmem((128, 256), f32),
        vmem((RANK, N), f32),
        dma,
        dma((3, 4)), dma((3, 4)), dma((2,)), dma((CHUNKS,)), dma((CHUNKS,)),
        dma((CHUNKS,)), dma((CHUNKS,)), dma((CHUNKS,)), dma((CHUNKS,)),
        dma((CHUNKS,)), dma((CHUNKS,)),
        dma((CHUNKS,)), dma((CHUNKS, CHIPS - 1)), dma((CHUNKS,)), dma((CHUNKS,)),
        pltpu.SemaphoreType.REGULAR((2, 4)),
    ]
    advanced, core, rebuilt = pl.pallas_call(
        functools.partial(kernel, rescale),
        out_shape=(
            jax.ShapeDtypeStruct(whole, f32),
            jax.ShapeDtypeStruct((F, 128), f32),
            jax.ShapeDtypeStruct(whole, f32),
        ),
        in_specs=[
            pl.BlockSpec(memory_space=pl.ANY),
            pl.BlockSpec(memory_space=pltpu.VMEM),
            pl.BlockSpec(memory_space=pltpu.VMEM),
        ],
        out_specs=[pl.BlockSpec(memory_space=pltpu.VMEM)] * 3,
        scratch_shapes=scratch,
        compiler_params=pltpu.CompilerParams(collective_id=0, has_side_effects=True),
        name="flow_tucker",
    )(fields, factor_x, factor_y)
    return advanced, core.reshape(F, 1, 1, 128), rebuilt


def solution(mesh):
    placed = P(None, "gx", "gy", None)
    return jax.shard_map(
        per_device,
        mesh=mesh,
        in_specs=(placed, P("gx", None), P("gy", None)),
        out_specs=(placed, placed, placed),
        check_vma=False,
    )
```

```python
import functools
import math

import jax
import jax.numpy as jnp
from jax import lax
from jax.experimental import pallas as pl
from jax.experimental.pallas import tpu as pltpu
from jax.sharding import PartitionSpec as P

TIME_STEP = 0.2
REACT_RATE = 0.5
HEAT_RELEASE = 1.0
HIGH = lax.Precision.HIGHEST
SECTIONS = ((0.0, 1.0), (0.75, 0.25), (1.0 / 3.0, 2.0 / 3.0))
LOW, TOP = 0, 1
N = 16
F = 4
VMEM_BYTES = 65500000
W = 3
RANK = 32
CHIPS = 16
CHUNKS = 2
FC = F // CHUNKS


def far_first(count):
    order = []
    for k in range(count // 2, 0, -1):
        order += [k] if 2 * k == count else [k, count - k]
    return order


Z_ORDER = far_first(32)


def in_plane_order():
    def hops(k):
        y, x = k % 4, k // 4
        return min(y, 4 - y) + min(x, 4 - x)

    return sorted(range(1, CHIPS), key=lambda k: -hops(k))


PLANE_ORDER = in_plane_order()


def iota(shape, dim):
    return lax.broadcasted_iota(jnp.int32, shape, dim)


def dot(a, b, contract=((1,), (0,))):
    return lax.dot_general(
        a, b, (contract, ((), ())), precision=HIGH, preferred_element_type=jnp.float32
    )


def one_hot(hit):
    return jnp.where(hit, 1.0, 0.0).astype(jnp.float32)


def spread(rows, cells):
    n, k = rows.shape
    wide = dot(rows, one_hot(iota((k, 8 * k), 1) // 8 == iota((k, 8 * k), 0)))
    same = iota((n, 8 * k), 0) % 8 == iota((n, 8 * k), 1) % 8
    return jnp.where(same, wide, 0.0)


def expand(lhs, columns, write):
    for i in range(FC):
        both = jnp.concatenate(
            [columns[:, i, 8 * t : 8 * t + 8, :].reshape(8 * RANK, 128) for t in range(2)], axis=1
        )
        whole = dot(lhs[...], both)
        for t in range(2):
            write(i, t, whole[:, 128 * t : 128 * t + 128].reshape(N, 8, 128))


def kernel(
    rescale,
    fields, fx_in, fy_in,
    adv, core_out, reb, last, lhs_out,
    state, flux_x, flux_y, halo_x, halo_y, edge_y,
    mate_adv, fx_own, fx_mate, part, part_in, local, core_in, core_own, core_all, cols, ahead,
    lhs_in, fy_t, fy,
    load_sem, factor_sems, halo_send, halo_recv, fx_sems, mate_send, mate_recv,
    plane_send, plane_recv, z_send, z_recv, zb_send, zb_recv, back_send, back_recv, pass_send, pass_recv,
    near_sem,
):
    gx, gy = lax.axis_index("gx"), lax.axis_index("gy")
    core = lax.rem(gx, 2)
    mate = {"gx": gx + 1 - 2 * core}

    def along(axis, offset):
        count, me = 32, (gx if axis == "gx" else gy)
        return {axis: lax.rem(me + (offset + count), count)}

    def signal(sem, target):
        pl.semaphore_signal(sem, inc=1, device_id=target, device_id_type=pl.DeviceIdType.MESH)

    def copy(src, dst, send, recv, target):
        return pltpu.make_async_remote_copy(
            src_ref=src, dst_ref=dst, send_sem=send, recv_sem=recv,
            device_id=target, device_id_type=pl.DeviceIdType.MESH,
        )

    def take_all(sem, ref):
        pltpu.make_async_copy(ref, ref, sem).wait()

    load = pltpu.make_async_copy(fields, state.at[0], load_sem)
    load.start()
    factors = [
        pltpu.make_async_copy(fx_in, fx_own, factor_sems.at[0]),
        pltpu.make_async_copy(fy_in, fy, factor_sems.at[1]),
    ]
    for c in factors:
        c.start()
    barrier = pltpu.get_barrier_semaphore()
    for axis in ("gx", "gy"):
        for side in (-1, 1):
            signal(barrier, along(axis, side))

    zero_rows = jnp.zeros((8, 128), jnp.float32)

    @pl.loop(0, N)
    def _(x):
        for f in range(F):
            flux_y[f, x, 0:8, :] = zero_rows
            flux_y[f, x, 24:32, :] = zero_rows

    pl.semaphore_wait(barrier, 4)

    def sign_in(level):
        for i, axis in enumerate(("gx", "gy")):
            for side in (-1, 1):
                signal(near_sem.at[i, level], along(axis, side * (1 << level)))

    def signed_in(level):
        for i in range(2):
            pl.semaphore_wait(near_sem.at[i, level], 2)

    sign_in(0)
    fx_copy = copy(fx_own, fx_mate, fx_sems.at[0], fx_sems.at[1], mate)
    for c in factors:
        c.wait()
    fx_copy.start()
    load.wait()

    def flat(s):
        return (adv if s == 3 else state.at[s]).reshape(F * N * N, 128)

    for f in range(F):
        for j in range(W):
            edge_y[0, LOW, f, j] = flat(0)[pl.ds(f * N * N + j, N, stride=N), :]
            edge_y[0, TOP, f, j] = flat(0)[pl.ds(f * N * N + N - W + j, N, stride=N), :]

    def halo_copies(s):
        now = state.at[s]
        return (
            copy(edge_y.at[s, LOW], halo_y.at[s, TOP], halo_send.at[s, 0], halo_recv.at[s, 0], along("gy", -1)),
            copy(edge_y.at[s, TOP], halo_y.at[s, LOW], halo_send.at[s, 1], halo_recv.at[s, 1], along("gy", 1)),
            copy(now.at[:, pl.ds(0, W)], halo_x.at[s, TOP], halo_send.at[s, 2], halo_recv.at[s, 2], along("gx", -1)),
            copy(now.at[:, pl.ds(N - W, W)], halo_x.at[s, LOW], halo_send.at[s, 3], halo_recv.at[s, 3], along("gx", 1)),
        )

    def fluxes(values, which):
        total = [values[which] * v for v in values]
        total[which] = total[which] + 0.5 * values[3]
        return total

    def prepare():
        fx_copy.wait_recv()
        picked = one_hot(iota((128, RANK), 1) == 2 * (iota((128, RANK), 0) // 8) + core)
        for half, factor in ((0, fx_own), (1, fx_mate)):
            rows = dot(picked, factor[...], ((1,), (1,)))
            lhs_in[:, 128 * half : 128 * half + 128] = spread(rows, N)
        rows = dot(one_hot(iota((128, N), 0) // 8 == iota((128, N), 1)), fx_own[...])
        lhs_out[...] = rescale * spread(rows, RANK)
        fy_t[...] = dot(one_hot(iota((RANK, RANK), 0) == iota((RANK, RANK), 1)), fy[...], ((1,), (1,)))

    def section(s):
        keep, take = SECTIONS[s]
        now, base = state.at[s], state.at[0]
        after = adv if s == 2 else state.at[s + 1]
        copies = halo_copies(s)
        for c in copies:
            c.start()

        @pl.loop(0, N)
        def _(x):
            for t in range(2):
                rows = pl.ds(8 * t, 8)
                values = [now[f, x, rows, :] for f in range(F)]
                for f, g in enumerate(fluxes(values, 0)):
                    flux_x[f, x + W, rows, :] = g
                for f, g in enumerate(fluxes(values, 1)):
                    flux_y[f, x, pl.ds(8 + 8 * t, 8), :] = g

        scale = take * TIME_STEP / 60.0

        def advance(x):
            for t in range(2):
                rows = pl.ds(8 * t, 8)
                heat = now[3, x, rows, :]
                react = (take * TIME_STEP * REACT_RATE) * now[2, x, rows, :] * (1.0 + jnp.tanh(heat))
                for f in range(F):
                    def pair(shift):
                        in_x = flux_x[f, x + (W + shift), rows, :] - flux_x[f, x + (W - shift), rows, :]
                        start = 8 + 8 * t
                        in_y = flux_y[f, x, pl.ds(start + shift, 8), :] - flux_y[f, x, pl.ds(start - shift, 8), :]
                        return in_x + in_y

                    slope = (45.0 * scale) * pair(1) - (9.0 * scale) * pair(2) + scale * pair(3)
                    new = take * now[f, x, rows, :] - slope
                    if keep:
                        new = new + keep * base[f, x, rows, :]
                    if f == 2:
                        new = new - react
                    if f == 3:
                        new = new + HEAT_RELEASE * react
                    after[f, x, rows, :] = new

        @pl.loop(W, N - W)
        def _(x):
            advance(x)

        if s < 2:
            signed_in(s)
            sign_in(s + 1)
        if s == 1:
            prepare()
        copies[2].wait_recv()
        copies[3].wait_recv()
        for side, first in ((LOW, 0), (TOP, N + W)):
            @pl.loop(0, W)
            def _(j):
                for t in range(2):
                    rows = pl.ds(8 * t, 8)
                    values = [halo_x[s, side, f, j, rows, :] for f in range(F)]
                    for f, g in enumerate(fluxes(values, 0)):
                        flux_x[f, first + j, rows, :] = g

        @pl.loop(0, W)
        def _(j):
            advance(j)
            advance(N - W + j)

        if s == 1:
            signed_in(2)
            sign_in(3)
        copies[0].wait_recv()
        copies[1].wait_recv()
        out = flat(s + 1)
        flux = []
        for side, near in ((LOW, (2, 1, 0)), (TOP, (0, 1, 2))):
            flux.append([fluxes([halo_y[s, side, f, j] for f in range(F)], 1) for j in near])
        for f in range(F):
            for side in (LOW, TOP):
                sign = 1.0 if side == LOW else -1.0
                g1, g2, g3 = (flux[side][k][f] for k in range(W))
                changes = (
                    (sign * 45.0 * scale) * g1 - (sign * 9.0 * scale) * g2 + (sign * scale) * g3,
                    (sign * scale) * g2 - (sign * 9.0 * scale) * g1,
                    (sign * scale) * g1,
                )
                for k, change in enumerate(changes):
                    y = k if side == LOW else N - 1 - k
                    at = pl.ds(f * N * N + y, N, stride=N)
                    new = out[at, :] + change
                    out[at, :] = new
                    if s < 2:
                        edge_y[s + 1, side, f, k if side == LOW else W - 1 - k] = new
            if s == 2 and (f + 1) % FC == 0:
                c = f // FC
                piece = pl.ds(c * FC, FC)
                mates.append(copy(adv.at[piece], mate_adv.at[piece], mate_send.at[c], mate_recv.at[c], mate))
                mates[-1].start()
        return copies

    mates = []
    sent = []
    sent += section(0)
    sent += section(1)
    sent += section(2)

    signed_in(3)
    sent += mates

    def tiles(ref, f):
        return jnp.concatenate(
            [ref[f, :, 8 * t : 8 * t + 8, :].reshape(8 * N, 128) for t in range(2)], axis=1
        )

    chip = gx // 2
    plane = []
    for c in range(CHUNKS):
        mates[c].wait_recv()
        for i in range(FC):
            f = c * FC + i
            both = jnp.concatenate([tiles(adv, f), tiles(mate_adv, f)], axis=0)
            total = dot(lhs_in[...], both)
            for t in range(2):
                part[c, :, i, 8 * t : 8 * t + 8, :] = total[:, 128 * t : 128 * t + 128].reshape(CHIPS, 8, 128)
        for k in PLANE_ORDER:
            to = lax.rem(chip + k, CHIPS)
            plane.append(
                copy(part.at[c, to], part_in.at[c, k - 1], plane_send.at[c], plane_recv.at[c], {"gx": 2 * to + core})
            )
            plane[-1].start()

    out_z = []
    for c in range(CHUNKS):
        take_all(plane_recv.at[c], part_in.at[c])
        for i in range(FC):
            total = part[c, chip, i]
            for k in range(CHIPS - 1):
                total = total + part_in[c, k, i]
            local[c, :, i, :] = dot(fy_t[...], total)
        for k in Z_ORDER:
            to = lax.rem(gy + k, 32)
            out_z.append(copy(local.at[c, to], core_in.at[c, k - 1], z_send.at[c], z_recv.at[c], {"gy": to}))
            out_z[-1].start()

    back_z = []
    for c in range(CHUNKS):
        take_all(z_recv.at[c], core_in.at[c])
        total = local[c, gy]
        for k in range(31):
            total = total + core_in[c, k]
        core_own[c] = total
        core_all[c, gy] = total
        core_out[c * FC : c * FC + FC] = total.reshape(FC, 1, 1, 128)
        for k in Z_ORDER:
            to = lax.rem(gy + k, 32)
            back_z.append(copy(core_own.at[c], core_all.at[c, gy], zb_send.at[c], zb_recv.at[c], {"gy": to}))
            back_z[-1].start()

    back = []
    passed = []
    gathered = [ahead.at[c] for c in range(CHUNKS - 1)] + [last]
    for c in range(CHUNKS):
        take_all(zb_recv.at[c], core_all.at[c, pl.ds(0, 31)])
        for i in range(FC):
            expanded = dot(fy[...], core_all[c, :, i, :])
            cols[c, i] = expanded
            gathered[c][gx, i] = expanded
        for k in PLANE_ORDER:
            to = lax.rem(chip + k, CHIPS)
            back.append(
                copy(cols.at[c], gathered[c].at[gx], back_send.at[c], back_recv.at[c, k - 1], {"gx": 2 * to + core})
            )
            back[-1].start()
        passed.append(copy(cols.at[c], gathered[c].at[gx], pass_send.at[c], pass_recv.at[c], mate))
        passed[-1].start()
    def settle(c):
        take_all(pass_recv.at[c], gathered[c].at[pl.ds(0, CHIPS)])

        def write(i, t, values):
            reb[c * FC + i, :, 8 * t : 8 * t + 8, :] = values

        expand(lhs_out, gathered[c], write)

    for c in range(CHUNKS):
        for n, k in reversed(list(enumerate(PLANE_ORDER))):
            back[c * (CHIPS - 1) + n].wait_recv()
            came = 2 * lax.rem(chip + (CHIPS - k), CHIPS) + core
            passed.append(
                copy(gathered[c].at[came], gathered[c].at[came], pass_send.at[c], pass_recv.at[c], mate)
            )
            passed[-1].start()
        if c > 0:
            settle(c - 1)
    take_all(pass_recv.at[CHUNKS - 1], last.at[pl.ds(0, CHIPS)])

    for c in sent + [fx_copy]:
        c.wait_send()
    for c in range(CHUNKS):
        take_all(plane_send.at[c], part_in.at[c])
        take_all(z_send.at[c], core_in.at[c])
        take_all(zb_send.at[c], core_all.at[c, pl.ds(0, 31)])
        take_all(back_send.at[c], last.at[pl.ds(0, CHIPS - 1)])
        take_all(pass_send.at[c], last.at[pl.ds(0, CHIPS)])


def finish(adv, core, reb, last, lhs_out, adv_out, core_out, reb_out, final, adv_sem, core_sem, reb_sem, final_sem):
    done = (CHUNKS - 1) * FC
    copies = [
        pltpu.make_async_copy(adv, adv_out, adv_sem),
        pltpu.make_async_copy(reb, reb_out.at[pl.ds(0, done)], reb_sem),
        pltpu.make_async_copy(core, core_out, core_sem),
    ]
    for c in copies:
        c.start()

    def write(i, t, values):
        final[i, :, 8 * t : 8 * t + 8, :] = values
        if t == 1:
            copies.append(pltpu.make_async_copy(final.at[i], reb_out.at[done + i], final_sem.at[i]))
            copies[-1].start()

    expand(lhs_out, last, write)
    for c in copies:
        c.wait()


def per_device(fields, factor_x, factor_y):
    total_x, total_y = factor_x.shape[0] * 32, factor_y.shape[0] * 32
    rescale = math.sqrt(float(total_x) * float(total_y)) / factor_x.shape[1]
    f32 = jnp.float32
    vmem = pltpu.VMEM
    dma = pltpu.SemaphoreType.DMA
    whole = (F, N, N, 128)
    scratch = [
        vmem((3, *whole), f32),
        vmem((F, N + 2 * W, N, 128), f32),
        vmem((F, N, 2 * N, 128), f32),
        vmem((3, 2, F, W, N, 128), f32),
        vmem((3, 2, F, W, N, 128), f32),
        vmem((3, 2, F, W, N, 128), f32),
        vmem(whole, f32),
        vmem((N, RANK), f32),
        vmem((N, RANK), f32),
        vmem((CHUNKS, CHIPS, FC, N, 128), f32),
        vmem((CHUNKS, CHIPS - 1, FC, N, 128), f32),
        vmem((CHUNKS, RANK, FC, 128), f32),
        vmem((CHUNKS, 31, FC, 128), f32),
        vmem((CHUNKS, FC, 128), f32),
        vmem((CHUNKS, RANK, FC, 128), f32),
        vmem((CHUNKS, FC, N, 128), f32),
        vmem((CHUNKS - 1, RANK, FC, N, 128), f32),
        vmem((128, 256), f32),
        vmem((RANK, N), f32),
        vmem((N, RANK), f32),
        dma,
        dma((2,)),
        dma((3, 4)), dma((3, 4)), dma((2,)), dma((CHUNKS,)), dma((CHUNKS,)),
        dma((CHUNKS,)), dma((CHUNKS,)), dma((CHUNKS,)), dma((CHUNKS,)),
        dma((CHUNKS,)), dma((CHUNKS,)),
        dma((CHUNKS,)), dma((CHUNKS, CHIPS - 1)), dma((CHUNKS,)), dma((CHUNKS,)),
        pltpu.SemaphoreType.REGULAR((2, 4)),
    ]
    inner = (whole, (F, 1, 1, 128), ((CHUNKS - 1) * FC, N, N, 128), (RANK, FC, N, 128), (128, 256))
    kept = pl.pallas_call(
        functools.partial(kernel, rescale),
        out_shape=[vmem(shape, f32) for shape in inner],
        in_specs=[
            pl.BlockSpec(memory_space=pltpu.HBM),
            pl.BlockSpec(memory_space=pltpu.HBM),
            pl.BlockSpec(memory_space=pltpu.HBM),
        ],
        out_specs=[pl.BlockSpec(memory_space=vmem)] * 5,
        scratch_shapes=scratch,
        compiler_params=pltpu.CompilerParams(collective_id=0, has_side_effects=True, vmem_limit_bytes=VMEM_BYTES),
        name="flow_tucker",
    )(fields, factor_x, factor_y)
    return pl.pallas_call(
        finish,
        out_shape=[jax.ShapeDtypeStruct(shape, f32) for shape in (whole, (F, 1, 1, 128), whole)],
        in_specs=[pl.BlockSpec(memory_space=vmem)] * 5,
        out_specs=[pl.BlockSpec(memory_space=pl.ANY)] * 3,
        scratch_shapes=[vmem((FC, N, N, 128), f32), dma, dma, dma, dma((FC,))],
        compiler_params=pltpu.CompilerParams(vmem_limit_bytes=4 << 20),
        name="expand_x",
    )(*kept)


def solution(mesh):
    placed = P(None, "gx", "gy", None)
    return jax.shard_map(
        per_device,
        mesh=mesh,
        in_specs=(placed, P("gx", None), P("gy", None)),
        out_specs=(placed, placed, placed),
        check_vma=False,
    )
```

```python
import functools
import math

import jax
import jax.numpy as jnp
from jax import lax
from jax.experimental import pallas as pl
from jax.experimental.pallas import tpu as pltpu
from jax.sharding import PartitionSpec as P

TIME_STEP = 0.2
REACT_RATE = 0.5
HEAT_RELEASE = 1.0
HIGH = lax.Precision.HIGHEST
SECTIONS = ((0.0, 1.0), (0.75, 0.25), (1.0 / 3.0, 2.0 / 3.0))
LOW, TOP = 0, 1
N = 16
F = 4
VMEM_BYTES = 65500000
W = 3
RANK = 32
CHIPS = 16
CHUNKS = 2
FC = F // CHUNKS


def far_first(count):
    order = []
    for k in range(count // 2, 0, -1):
        order += [k] if 2 * k == count else [k, count - k]
    return order


Z_ORDER = far_first(32)


def in_plane_order():
    def hops(k):
        y, x = k % 4, k // 4
        return min(y, 4 - y) + min(x, 4 - x)

    return sorted(range(1, CHIPS), key=lambda k: -hops(k))


PLANE_ORDER = in_plane_order()


def iota(shape, dim):
    return lax.broadcasted_iota(jnp.int32, shape, dim)


def dot(a, b, contract=((1,), (0,))):
    return lax.dot_general(
        a, b, (contract, ((), ())), precision=HIGH, preferred_element_type=jnp.float32
    )


def one_hot(hit):
    return jnp.where(hit, 1.0, 0.0).astype(jnp.float32)


def spread(rows, cells):
    n, k = rows.shape
    wide = dot(rows, one_hot(iota((k, 8 * k), 1) // 8 == iota((k, 8 * k), 0)))
    same = iota((n, 8 * k), 0) % 8 == iota((n, 8 * k), 1) % 8
    return jnp.where(same, wide, 0.0)


def expand(lhs, columns, write):
    for i in range(FC):
        both = jnp.concatenate(
            [columns[:, i, 8 * t : 8 * t + 8, :].reshape(8 * RANK, 128) for t in range(2)], axis=1
        )
        whole = dot(lhs[...], both)
        for t in range(2):
            write(i, t, whole[:, 128 * t : 128 * t + 128].reshape(N, 8, 128))


def kernel(
    rescale,
    fields, fx_in, fy_in,
    adv, core_out, reb, last, lhs_out,
    state, flux_x, flux_y, halo_x, halo_y, edge_y,
    mate_adv, fx_own, fx_mate, part, part_in, local, core_in, core_own, core_all, cols, ahead,
    lhs_in, fy_t, fy,
    load_sem, factor_sems, halo_send, halo_recv, fx_sems, mate_send, mate_recv,
    plane_send, plane_recv, z_send, z_recv, zb_send, zb_recv, back_send, back_recv, pass_send, pass_recv,
    near_sem,
):
    gx, gy = lax.axis_index("gx"), lax.axis_index("gy")
    core = lax.rem(gx, 2)
    mate = {"gx": gx + 1 - 2 * core}

    def along(axis, offset):
        count, me = 32, (gx if axis == "gx" else gy)
        return {axis: lax.rem(me + (offset + count), count)}

    def signal(sem, target):
        pl.semaphore_signal(sem, inc=1, device_id=target, device_id_type=pl.DeviceIdType.MESH)

    def copy(src, dst, send, recv, target):
        return pltpu.make_async_remote_copy(
            src_ref=src, dst_ref=dst, send_sem=send, recv_sem=recv,
            device_id=target, device_id_type=pl.DeviceIdType.MESH,
        )

    def take_all(sem, ref):
        pltpu.make_async_copy(ref, ref, sem).wait()

    loads = [pltpu.make_async_copy(fields.at[f], state.at[0, f], load_sem.at[f]) for f in range(F)]
    for c in loads:
        c.start()
    factors = [
        pltpu.make_async_copy(fx_in, fx_own, factor_sems.at[0]),
        pltpu.make_async_copy(fy_in, fy, factor_sems.at[1]),
    ]
    for c in factors:
        c.start()
    barrier = pltpu.get_barrier_semaphore()
    for axis in ("gx", "gy"):
        for side in (-1, 1):
            signal(barrier, along(axis, side))

    zero_rows = jnp.zeros((8, 128), jnp.float32)

    @pl.loop(0, N)
    def _(x):
        for f in range(F):
            flux_y[f, x, 0:8, :] = zero_rows
            flux_y[f, x, 24:32, :] = zero_rows

    pl.semaphore_wait(barrier, 4)

    def sign_in(level):
        for i, axis in enumerate(("gx", "gy")):
            for side in (-1, 1):
                signal(near_sem.at[i, level], along(axis, side * (1 << level)))

    def signed_in(level):
        for i in range(2):
            pl.semaphore_wait(near_sem.at[i, level], 2)

    sign_in(0)
    fx_copy = copy(fx_own, fx_mate, fx_sems.at[0], fx_sems.at[1], mate)
    for c in factors:
        c.wait()
    fx_copy.start()

    def flat(s):
        return (adv if s == 3 else state.at[s]).reshape(F * N * N, 128)

    def send_edges(s, f):
        now = state.at[s, f]
        for k, (src, dst, axis, step) in enumerate((
            (edge_y.at[s, LOW, f], halo_y.at[s, TOP, f], "gy", -1),
            (edge_y.at[s, TOP, f], halo_y.at[s, LOW, f], "gy", 1),
            (now.at[pl.ds(0, W)], halo_x.at[s, TOP, f], "gx", -1),
            (now.at[pl.ds(N - W, W)], halo_x.at[s, LOW, f], "gx", 1),
        )):
            copy(src, dst, halo_send.at[s, k], halo_recv.at[s, k], along(axis, step)).start()

    for f in range(F):
        loads[f].wait()
        for j in range(W):
            edge_y[0, LOW, f, j] = flat(0)[pl.ds(f * N * N + j, N, stride=N), :]
            edge_y[0, TOP, f, j] = flat(0)[pl.ds(f * N * N + N - W + j, N, stride=N), :]
        if f:
            send_edges(0, f - 1)
    send_edges(0, F - 1)

    def fluxes(values, which):
        total = [values[which] * v for v in values]
        total[which] = total[which] + 0.5 * values[3]
        return total

    def prepare():
        fx_copy.wait_recv()
        picked = one_hot(iota((128, RANK), 1) == 2 * (iota((128, RANK), 0) // 8) + core)
        for half, factor in ((0, fx_own), (1, fx_mate)):
            rows = dot(picked, factor[...], ((1,), (1,)))
            lhs_in[:, 128 * half : 128 * half + 128] = spread(rows, N)
        rows = dot(one_hot(iota((128, N), 0) // 8 == iota((128, N), 1)), fx_own[...])
        lhs_out[...] = rescale * spread(rows, RANK)
        fy_t[...] = dot(one_hot(iota((RANK, RANK), 0) == iota((RANK, RANK), 1)), fy[...], ((1,), (1,)))

    def hand_on(s, f):
        if s < 2:
            send_edges(s + 1, f)
        else:
            mates.append(copy(adv.at[f], mate_adv.at[f], mate_send.at[f], mate_recv.at[f], mate))
            mates[-1].start()

    def section(s):
        keep, take = SECTIONS[s]
        now, base = state.at[s], state.at[0]
        after = adv if s == 2 else state.at[s + 1]
        @pl.loop(0, N)
        def _(x):
            for t in range(2):
                rows = pl.ds(8 * t, 8)
                values = [now[f, x, rows, :] for f in range(F)]
                for f, g in enumerate(fluxes(values, 0)):
                    flux_x[f, x + W, rows, :] = g
                for f, g in enumerate(fluxes(values, 1)):
                    flux_y[f, x, pl.ds(8 + 8 * t, 8), :] = g

        scale = take * TIME_STEP / 60.0

        def advance(x):
            for t in range(2):
                rows = pl.ds(8 * t, 8)
                heat = now[3, x, rows, :]
                react = (take * TIME_STEP * REACT_RATE) * now[2, x, rows, :] * (1.0 + jnp.tanh(heat))
                for f in range(F):
                    def pair(shift):
                        in_x = flux_x[f, x + (W + shift), rows, :] - flux_x[f, x + (W - shift), rows, :]
                        start = 8 + 8 * t
                        in_y = flux_y[f, x, pl.ds(start + shift, 8), :] - flux_y[f, x, pl.ds(start - shift, 8), :]
                        return in_x + in_y

                    slope = (45.0 * scale) * pair(1) - (9.0 * scale) * pair(2) + scale * pair(3)
                    new = take * now[f, x, rows, :] - slope
                    if keep:
                        new = new + keep * base[f, x, rows, :]
                    if f == 2:
                        new = new - react
                    if f == 3:
                        new = new + HEAT_RELEASE * react
                    after[f, x, rows, :] = new

        @pl.loop(W, N - W)
        def _(x):
            advance(x)

        if s < 2:
            signed_in(s)
            sign_in(s + 1)
        if s == 1:
            prepare()
        take_all(halo_recv.at[s, 2], halo_x.at[s, TOP])
        take_all(halo_recv.at[s, 3], halo_x.at[s, LOW])
        for side, first in ((LOW, 0), (TOP, N + W)):
            @pl.loop(0, W)
            def _(j):
                for t in range(2):
                    rows = pl.ds(8 * t, 8)
                    values = [halo_x[s, side, f, j, rows, :] for f in range(F)]
                    for f, g in enumerate(fluxes(values, 0)):
                        flux_x[f, first + j, rows, :] = g

        @pl.loop(0, W)
        def _(j):
            advance(j)
            advance(N - W + j)

        if s == 1:
            signed_in(2)
            sign_in(3)
        take_all(halo_recv.at[s, 0], halo_y.at[s, TOP])
        take_all(halo_recv.at[s, 1], halo_y.at[s, LOW])
        out = flat(s + 1)
        flux = []
        for side, near in ((LOW, (2, 1, 0)), (TOP, (0, 1, 2))):
            flux.append([fluxes([halo_y[s, side, f, j] for f in range(F)], 1) for j in near])
        for f in range(F):
            for side in (LOW, TOP):
                sign = 1.0 if side == LOW else -1.0
                g1, g2, g3 = (flux[side][k][f] for k in range(W))
                changes = (
                    (sign * 45.0 * scale) * g1 - (sign * 9.0 * scale) * g2 + (sign * scale) * g3,
                    (sign * scale) * g2 - (sign * 9.0 * scale) * g1,
                    (sign * scale) * g1,
                )
                for k, change in enumerate(changes):
                    y = k if side == LOW else N - 1 - k
                    at = pl.ds(f * N * N + y, N, stride=N)
                    new = out[at, :] + change
                    out[at, :] = new
                    if s < 2:
                        edge_y[s + 1, side, f, k if side == LOW else W - 1 - k] = new
            if f:
                hand_on(s, f - 1)
        hand_on(s, F - 1)

    mates = []
    for s in range(3):
        section(s)

    signed_in(3)

    def tiles(ref, f):
        return jnp.concatenate(
            [ref[f, :, 8 * t : 8 * t + 8, :].reshape(8 * N, 128) for t in range(2)], axis=1
        )

    chip = gx // 2
    for c in range(CHUNKS):
        for i in range(FC):
            f = c * FC + i
            mates[f].wait_recv()
            both = jnp.concatenate([tiles(adv, f), tiles(mate_adv, f)], axis=0)
            total = dot(lhs_in[...], both)
            for t in range(2):
                part[c, :, i, 8 * t : 8 * t + 8, :] = total[:, 128 * t : 128 * t + 128].reshape(CHIPS, 8, 128)
            for k in PLANE_ORDER:
                to = lax.rem(chip + k, CHIPS)
                copy(
                    part.at[c, to, i], part_in.at[c, k - 1, i], plane_send.at[c], plane_recv.at[c],
                    {"gx": 2 * to + core},
                ).start()

    out_z = []
    for c in range(CHUNKS):
        take_all(plane_recv.at[c], part_in.at[c])
        for i in range(FC):
            total = part[c, chip, i]
            for k in range(CHIPS - 1):
                total = total + part_in[c, k, i]
            local[c, :, i, :] = dot(fy_t[...], total)
        for k in Z_ORDER:
            to = lax.rem(gy + k, 32)
            out_z.append(copy(local.at[c, to], core_in.at[c, k - 1], z_send.at[c], z_recv.at[c], {"gy": to}))
            out_z[-1].start()

    back_z = []
    for c in range(CHUNKS):
        take_all(z_recv.at[c], core_in.at[c])
        total = local[c, gy]
        for k in range(31):
            total = total + core_in[c, k]
        core_own[c] = total
        core_all[c, gy] = total
        core_out[c * FC : c * FC + FC] = total.reshape(FC, 1, 1, 128)
        for k in Z_ORDER:
            to = lax.rem(gy + k, 32)
            back_z.append(copy(core_own.at[c], core_all.at[c, gy], zb_send.at[c], zb_recv.at[c], {"gy": to}))
            back_z[-1].start()

    back = []
    passed = []
    gathered = [ahead.at[c] for c in range(CHUNKS - 1)] + [last]
    for c in range(CHUNKS):
        take_all(zb_recv.at[c], core_all.at[c, pl.ds(0, 31)])
        for i in range(FC):
            expanded = dot(fy[...], core_all[c, :, i, :])
            cols[c, i] = expanded
            gathered[c][gx, i] = expanded
        for k in PLANE_ORDER:
            to = lax.rem(chip + k, CHIPS)
            back.append(
                copy(cols.at[c], gathered[c].at[gx], back_send.at[c], back_recv.at[c, k - 1], {"gx": 2 * to + core})
            )
            back[-1].start()
        passed.append(copy(cols.at[c], gathered[c].at[gx], pass_send.at[c], pass_recv.at[c], mate))
        passed[-1].start()
    def settle(c):
        take_all(pass_recv.at[c], gathered[c].at[pl.ds(0, CHIPS)])

        def write(i, t, values):
            reb[c * FC + i, :, 8 * t : 8 * t + 8, :] = values

        expand(lhs_out, gathered[c], write)

    for c in range(CHUNKS):
        for n, k in reversed(list(enumerate(PLANE_ORDER))):
            back[c * (CHIPS - 1) + n].wait_recv()
            came = 2 * lax.rem(chip + (CHIPS - k), CHIPS) + core
            passed.append(
                copy(gathered[c].at[came], gathered[c].at[came], pass_send.at[c], pass_recv.at[c], mate)
            )
            passed[-1].start()
        if c > 0:
            settle(c - 1)
    take_all(pass_recv.at[CHUNKS - 1], last.at[pl.ds(0, CHIPS)])

    for c in mates + [fx_copy]:
        c.wait_send()
    for s in range(3):
        for k in range(4):
            take_all(halo_send.at[s, k], halo_y.at[s, k // 2])
    for c in range(CHUNKS):
        take_all(plane_send.at[c], part_in.at[c])
        take_all(z_send.at[c], core_in.at[c])
        take_all(zb_send.at[c], core_all.at[c, pl.ds(0, 31)])
        take_all(back_send.at[c], last.at[pl.ds(0, CHIPS - 1)])
        take_all(pass_send.at[c], last.at[pl.ds(0, CHIPS)])


def finish(adv, core, reb, last, lhs_out, adv_out, core_out, reb_out, final, adv_sem, core_sem, reb_sem, final_sem):
    done = (CHUNKS - 1) * FC
    copies = [
        pltpu.make_async_copy(adv, adv_out, adv_sem),
        pltpu.make_async_copy(reb, reb_out.at[pl.ds(0, done)], reb_sem),
        pltpu.make_async_copy(core, core_out, core_sem),
    ]
    for c in copies:
        c.start()

    def write(i, t, values):
        final[i, :, 8 * t : 8 * t + 8, :] = values
        if t == 1:
            copies.append(pltpu.make_async_copy(final.at[i], reb_out.at[done + i], final_sem.at[i]))
            copies[-1].start()

    expand(lhs_out, last, write)
    for c in copies:
        c.wait()


def per_device(fields, factor_x, factor_y):
    total_x, total_y = factor_x.shape[0] * 32, factor_y.shape[0] * 32
    rescale = math.sqrt(float(total_x) * float(total_y)) / factor_x.shape[1]
    f32 = jnp.float32
    vmem = pltpu.VMEM
    dma = pltpu.SemaphoreType.DMA
    whole = (F, N, N, 128)
    scratch = [
        vmem((3, *whole), f32),
        vmem((F, N + 2 * W, N, 128), f32),
        vmem((F, N, 2 * N, 128), f32),
        vmem((3, 2, F, W, N, 128), f32),
        vmem((3, 2, F, W, N, 128), f32),
        vmem((3, 2, F, W, N, 128), f32),
        vmem(whole, f32),
        vmem((N, RANK), f32),
        vmem((N, RANK), f32),
        vmem((CHUNKS, CHIPS, FC, N, 128), f32),
        vmem((CHUNKS, CHIPS - 1, FC, N, 128), f32),
        vmem((CHUNKS, RANK, FC, 128), f32),
        vmem((CHUNKS, 31, FC, 128), f32),
        vmem((CHUNKS, FC, 128), f32),
        vmem((CHUNKS, RANK, FC, 128), f32),
        vmem((CHUNKS, FC, N, 128), f32),
        vmem((CHUNKS - 1, RANK, FC, N, 128), f32),
        vmem((128, 256), f32),
        vmem((RANK, N), f32),
        vmem((N, RANK), f32),
        dma((F,)),
        dma((2,)),
        dma((3, 4)), dma((3, 4)), dma((2,)), dma((F,)), dma((F,)),
        dma((CHUNKS,)), dma((CHUNKS,)), dma((CHUNKS,)), dma((CHUNKS,)),
        dma((CHUNKS,)), dma((CHUNKS,)),
        dma((CHUNKS,)), dma((CHUNKS, CHIPS - 1)), dma((CHUNKS,)), dma((CHUNKS,)),
        pltpu.SemaphoreType.REGULAR((2, 4)),
    ]
    inner = (whole, (F, 1, 1, 128), ((CHUNKS - 1) * FC, N, N, 128), (RANK, FC, N, 128), (128, 256))
    kept = pl.pallas_call(
        functools.partial(kernel, rescale),
        out_shape=[vmem(shape, f32) for shape in inner],
        in_specs=[
            pl.BlockSpec(memory_space=pltpu.HBM),
            pl.BlockSpec(memory_space=pltpu.HBM),
            pl.BlockSpec(memory_space=pltpu.HBM),
        ],
        out_specs=[pl.BlockSpec(memory_space=vmem)] * 5,
        scratch_shapes=scratch,
        compiler_params=pltpu.CompilerParams(collective_id=0, has_side_effects=True, vmem_limit_bytes=VMEM_BYTES),
        name="flow_tucker",
    )(fields, factor_x, factor_y)
    return pl.pallas_call(
        finish,
        out_shape=[jax.ShapeDtypeStruct(shape, f32) for shape in (whole, (F, 1, 1, 128), whole)],
        in_specs=[pl.BlockSpec(memory_space=vmem)] * 5,
        out_specs=[pl.BlockSpec(memory_space=pl.ANY)] * 3,
        scratch_shapes=[vmem((FC, N, N, 128), f32), dma, dma, dma, dma((FC,))],
        compiler_params=pltpu.CompilerParams(vmem_limit_bytes=4 << 20),
        name="expand_x",
    )(*kept)


def solution(mesh):
    placed = P(None, "gx", "gy", None)
    return jax.shard_map(
        per_device,
        mesh=mesh,
        in_specs=(placed, P("gx", None), P("gy", None)),
        out_specs=(placed, placed, placed),
        check_vma=False,
    )
```
